128 devices in a mesh: wide: 32 (over y_lo, x, z), narrow: 4 (over y_hi, core).
Axes of the slice: x: 4, y: 4 (y_hi: 2, y_lo: 2; y = y_hi * 2 + y_lo), z: 4, core: 2. Of those that a mesh axis runs over, the one named last changes fastest.
Arguments:
- pos_factor: float32 [1024, 131072], P('wide', 'narrow'), may hold values from -6 to 6
- vel_factor: float32 [1024, 131072], P('wide', 'narrow'), may hold values from -6 to 6
- stiff_vals: float32 [4, 512, 64, 256], P('narrow', 'wide'), may hold values from -0.375 to 0.375
- stiff_pattern: int32 [4, 512, 4], P('narrow', 'wide'), may hold values from 0 to 19
- mass_vals: float32 [4, 512, 64, 256], P('narrow', 'wide'), may hold values from -0.375 to 0.375
- mass_pattern: int32 [4, 512, 4], P('narrow', 'wide'), may hold values from 0 to 19
- interface: int32 [4, 32, 2, 2], P('narrow', 'wide'), may hold values from 0 to 15
Outputs:
- cross_tiles: float32 [1024, 1024], P(('wide', 'narrow'))
The draws below stay inside these ranges and needn't reach their ends.
All inputs are finite; a program needn't handle non-finite values.
Results may differ from the reference program's by a relative error of at most 0.0001.
Values sent between devices are 32-bit elements; how exact they have to be, the bound alone decides.
A program may use at most 128 MiB of HBM per device.

```python
import jax
import jax.numpy as jnp
from jax import lax

FACTOR_COLUMNS = 1024
BLOCK_DOFS = 64
PART_BLOCKS = 16
NB = 4
H = 2
GROUPS = 4
SLICES = 32
EXT = 20
NROWS = 131072


def set_ends(array, own_key, least, largest):
    dims = array.shape
    spot = [jax.random.randint(jax.random.fold_in(own_key, axis), (), 0, dims[axis]) for axis in range(len(dims))]
    array = array.at[tuple(spot)].set(least)
    longest = dims.index(max(dims))
    spot[longest] = (spot[longest] + 1) % dims[longest]
    return array.at[tuple(spot)].set(largest)


def block_scale(stream_key, extent, shards, smallest, top_value):
    factor_of, own = 1.0, jax.random.fold_in(stream_key, 6)
    for dim, shards_of in shards:
        heights = jnp.exp(jax.random.uniform(jax.random.fold_in(own, dim), (shards_of,), jnp.float32, smallest / len(shards), top_value / len(shards)))
        factor_of = factor_of * jnp.repeat(heights, extent[dim] // shards_of).reshape([-1 if axis == dim else 1 for axis in range(len(extent))])
    return factor_of


def noise(own_key, shape, deviation, bound, pieces=(), held_as=jnp.bfloat16):
    values = jax.random.normal(own_key, shape, jnp.float32) * deviation
    if len(pieces) > 0:
        values = block_scale(own_key, shape, pieces, -0.22, 0.18) * values
    return jnp.clip(values, min=-bound, max=bound).astype(held_as)


def setup_inputs(seed: int = 0) -> dict:
    key_list = jax.random.split(jax.random.key(seed), 8)
    return {
        "pos_factor": noise(key_list[0], (FACTOR_COLUMNS, NROWS), 1.0, 6.0, ((0, 32), (1, 4)), jnp.float32),
        "vel_factor": noise(key_list[1], (FACTOR_COLUMNS, NROWS), 1.0, 6.0, ((0, 32), (1, 4)), jnp.float32),
        "stiff_vals": noise(key_list[2], (GROUPS, SLICES * PART_BLOCKS, BLOCK_DOFS, NB * BLOCK_DOFS), (NB * BLOCK_DOFS) ** -0.5, 0.375, ((0, 4), (1, 32)), jnp.float32),
        "stiff_pattern": set_ends(jax.random.randint(key_list[3], (GROUPS, SLICES * PART_BLOCKS, NB), 0, EXT), jax.random.fold_in(key_list[3], 1), 0, EXT - 1).astype(jnp.int32),
        "mass_vals": noise(key_list[4], (GROUPS, SLICES * PART_BLOCKS, BLOCK_DOFS, NB * BLOCK_DOFS), (NB * BLOCK_DOFS) ** -0.5, 0.375, ((0, 4), (1, 32)), jnp.float32),
        "mass_pattern": set_ends(jax.random.randint(key_list[5], (GROUPS, SLICES * PART_BLOCKS, NB), 0, EXT), jax.random.fold_in(key_list[5], 1), 0, EXT - 1).astype(jnp.int32),
        "interface": set_ends(jax.random.randint(key_list[6], (GROUPS, SLICES, 2, H), 0, PART_BLOCKS), jax.random.fold_in(key_list[6], 1), 0, PART_BLOCKS - 1).astype(jnp.int32),
    }


def take_blocks(blocks, picks):
    return jax.vmap(jax.vmap(lambda field, index: field[index]))(blocks, picks)

def rim_sets(blocks, interface):
    upward = take_blocks(blocks, interface[:, :, 0])
    downward = take_blocks(blocks, interface[:, :, 1])
    empty = jnp.zeros_like(upward[:1])
    lower = jnp.concatenate([empty, upward[:-1]], 0)
    upper = jnp.concatenate([downward[1:], empty], 0)
    return (lower, upper)

def apply_block_matrix(values, pattern, extended):
    total = jnp.zeros((PART_BLOCKS, BLOCK_DOFS, FACTOR_COLUMNS), jnp.float32)
    for k in range(NB):
        total = total + jnp.einsum('bij,bjr->bir', values[:, k], extended[pattern[:, k]], precision=lax.Precision.HIGHEST)
    return total

def reference(pos_factor, vel_factor, stiff_vals, stiff_pattern, mass_vals, mass_pattern, interface):
    count = GROUPS * SLICES
    pos_blocks = pos_factor.T.reshape(GROUPS, SLICES, PART_BLOCKS, BLOCK_DOFS, FACTOR_COLUMNS)
    vel_blocks = vel_factor.T.reshape(GROUPS, SLICES, PART_BLOCKS, BLOCK_DOFS, FACTOR_COLUMNS)
    pos_lower, pos_upper = rim_sets(pos_blocks, interface)
    vel_lower, vel_upper = rim_sets(vel_blocks, interface)
    flat = lambda a: a.reshape((count,) + a.shape[2:])
    stiff = stiff_vals.reshape(count, PART_BLOCKS, BLOCK_DOFS, NB, BLOCK_DOFS).transpose(0, 1, 3, 2, 4)
    mass = mass_vals.reshape(count, PART_BLOCKS, BLOCK_DOFS, NB, BLOCK_DOFS).transpose(0, 1, 3, 2, 4)
    stiff_idx = stiff_pattern.reshape(count, PART_BLOCKS, NB)
    mass_idx = mass_pattern.reshape(count, PART_BLOCKS, NB)
    inputs = (flat(pos_blocks), flat(pos_lower), flat(pos_upper), flat(vel_blocks), flat(vel_lower), flat(vel_upper), stiff, stiff_idx, mass, mass_idx)

    def step(carry, item):
        pblk, plow, pupp, velocity_block_rows, velocity_lower_rim, velocity_upper_rim, kval, kidx, mass_block_values, mass_block_index = item
        pext = jnp.concatenate([plow, pblk, pupp], 0)
        velocity_extended = jnp.concatenate([velocity_lower_rim, velocity_block_rows, velocity_upper_rim], 0)
        moved = apply_block_matrix(kval, kidx, pext).reshape(PART_BLOCKS * BLOCK_DOFS, FACTOR_COLUMNS)
        velocity_local = apply_block_matrix(mass_block_values, mass_block_index, velocity_extended).reshape(PART_BLOCKS * BLOCK_DOFS, FACTOR_COLUMNS)
        term = lax.dot_general(moved, velocity_local, (((0,), (0,)), ((), ())), precision=lax.Precision.HIGHEST, preferred_element_type=jnp.float32)
        return (carry + term, None)
    total, _ = lax.scan(step, jnp.zeros((FACTOR_COLUMNS, FACTOR_COLUMNS), jnp.float32), inputs)
    return total / jnp.sqrt(jnp.float32(NROWS))
```

```python
import functools
import math

import jax
import jax.numpy as jnp
from jax import lax
from jax.experimental import pallas as pl
from jax.experimental.pallas import tpu as pltpu
from jax.sharding import PartitionSpec as P

MESH = pl.DeviceIdType.MESH
X_SIDE = 4
Z_SIDE = 4
LANES = 128

PAIRS = (
    (1, 1), (2, 3), (0, 2), (3, 0),
    (3, 3), (1, 2), (0, 1), (2, 0),
    (2, 2), (3, 1), (0, 3), (1, 0),
    (1, 3), (2, 1), (3, 2), (0, 0),
)
SHIFTS = tuple((dy, dx, dz) for dx, dz in PAIRS for dy in (0, 1))
CHUNK = 8


def two_halves(value):
    high = value.astype(jnp.bfloat16)
    low = (value - high.astype(jnp.float32)).astype(jnp.bfloat16)
    return high, low


def dot_t(a, b):
    return lax.dot_general(a, b, (((1,), (1,)), ((), ())), preferred_element_type=jnp.float32)


def dot3(ah, al, bh, bl):
    return dot_t(ah, bh) + (dot_t(ah, bl) + dot_t(al, bh))


def kernel(
    scale, pos_ref, vel_ref, stiff_ref, stiff_pat, mass_ref, mass_pat, picks, out_ref,
    pos_in, vel_in, halo, halo_out, stiff_h, stiff_l, mass_h, mass_l, e_h, e_l, p_f, p_h, p_l, v_h, v_l,
    x_out, x_in, y_out, y_in, z_out, z_in,
    send_sem, recv_sem, own_sem, halo_send, halo_recv, x_send, x_recv, y_send, y_recv, z_send, z_recv,
):
    wide = lax.axis_index("wide")
    narrow = lax.axis_index("narrow")
    plane = X_SIDE * Z_SIDE
    me_y, me_x, me_z = wide // plane, (wide // Z_SIDE) % X_SIDE, wide % Z_SIDE
    core, high_y = narrow % 2, narrow // 2
    slots = len(SHIFTS)
    chunks = slots // CHUNK
    cols, dofs = pos_in.shape[1], pos_in.shape[2]
    rows = CHUNK * cols
    blocks = mass_ref.shape[1]
    size = mass_ref.shape[2]

    def to(shift):
        dy, dx, dz = shift
        return ((me_y + dy) % 2) * plane + ((me_x + dx) % X_SIDE) * Z_SIDE + (me_z + dz) % Z_SIDE

    def back(shift):
        dy, dx, dz = shift
        return to((dy, (X_SIDE - dx) % X_SIDE, (Z_SIDE - dz) % Z_SIDE))

    core_partner = {"narrow": narrow + 1 - 2 * core}
    y_partner = {"wide": (wide + plane) % (2 * plane), "narrow": (narrow + 2) % 4}

    barrier = pltpu.get_barrier_semaphore()
    for shift in SHIFTS:
        if shift != (0, 0, 0):
            pl.semaphore_signal(barrier, inc=1, device_id={"wide": to(shift)}, device_id_type=MESH)
    for step in (1, 2, 3):
        pl.semaphore_signal(barrier, inc=1, device_id={"narrow": (narrow + step) % 4}, device_id_type=MESH)
    pl.semaphore_signal(barrier, inc=1, device_id=y_partner, device_id_type=MESH)
    pl.semaphore_wait(barrier, slots - 1 + 3 + 1)

    def exchange(which, slot):
        shift = SHIFTS[slot]
        source = (vel_ref, pos_ref)[which]
        target = to(shift)
        view = source.at[:, pl.ds(pl.multiple_of(target * dofs, dofs), dofs)]
        into = vel_in.at[wide] if which == 0 else pos_in.at[slot]
        if shift == (0, 0, 0):
            return pltpu.make_async_copy(view, into, own_sem.at[which])
        return pltpu.make_async_remote_copy(
            src_ref=view, dst_ref=into, send_sem=send_sem.at[which, slot], recv_sem=recv_sem.at[which, slot],
            device_id={"wide": target}, device_id_type=MESH,
        )

    copies = [[exchange(which, slot) for slot in range(slots)] for which in range(2)]
    for group in copies:
        for copy in group:
            copy.start()

    def arrived(which, slot):
        copy = copies[which][slot]
        if SHIFTS[slot] == (0, 0, 0):
            copy.wait()
        else:
            copy.wait_recv()

    lane = lax.broadcasted_iota(jnp.int32, (1, LANES), 1)
    left = lane < size
    half = lane // size

    def build(values, pattern, into_h, into_l):
        def row(b, carry):
            tiles = [values[0, b, :, t * LANES:(t + 1) * LANES] for t in range(2)]
            turned = [pltpu.roll(t, size, 1) for t in tiles]
            twice = []
            for t in range(2):
                twice.append(jnp.where(left, tiles[t], turned[t]))
                twice.append(jnp.where(left, turned[t], tiles[t]))
            at = pl.ds(pl.multiple_of(b * size, size), size)
            for pair in range(into_h.shape[1] // LANES):
                total = jnp.zeros((size, LANES), jnp.float32)
                for k in range(4):
                    total = total + jnp.where(half == pattern[0, b, k] - 2 * pair, twice[k], 0.0)
                h, l = two_halves(total)
                into_h[at, pair * LANES:(pair + 1) * LANES] = h
                into_l[at, pair * LANES:(pair + 1) * LANES] = l
            return carry

        lax.fori_loop(0, blocks, row, 0)

    build(mass_ref, mass_pat, mass_h, mass_l)
    build(stiff_ref, stiff_pat, stiff_h, stiff_l)

    @pl.when(narrow == 0)
    def _():
        halo[:, 0] = jnp.zeros(halo.shape[:1] + halo.shape[2:], jnp.float32)

    @pl.when(narrow == 3)
    def _():
        halo[:, 1] = jnp.zeros(halo.shape[:1] + halo.shape[2:], jnp.float32)

    wanted = [jnp.where(left, picks[0, 0, way, 0], picks[0, 0, way, 1]) for way in range(2)]

    def pick(field, which, q):
        def one(i, carry):
            found = [jnp.zeros((cols, LANES), jnp.float32)] * 2
            for t in range(dofs // LANES):
                tile = field[q * CHUNK + i, :, t * LANES:(t + 1) * LANES]
                turned = pltpu.roll(tile, size, 1)
                twice = (jnp.where(left, tile, turned), jnp.where(left, turned, tile))
                for way in range(2):
                    for h in range(2):
                        found[way] = jnp.where(wanted[way] == 2 * t + h, twice[h], found[way])
            for way in range(2):
                halo_out[which, way, q, pl.ds(pl.multiple_of(i * cols, cols), cols)] = found[way]
            return carry
        lax.fori_loop(0, CHUNK, one, 0)

    def halo_copy(which, q, way):
        return pltpu.make_async_remote_copy(
            src_ref=halo_out.at[which, way, q], dst_ref=halo.at[which, way, q],
            send_sem=halo_send.at[which, way, q], recv_sem=halo_recv.at[which, way, q],
            device_id={"narrow": (narrow + (1 if way == 0 else 3)) % 4}, device_id_type=MESH,
        )

    def send_halo(field, which, q):
        pick(field, which, q)
        for way in range(2):
            @pl.when(narrow != (3 if way == 0 else 0))
            def _():
                halo_copy(which, q, way).start()

    def take_halo(which, q):
        for way in range(2):
            @pl.when(narrow != (0 if way == 0 else 3))
            def _():
                halo_copy(which, q, way).wait_recv()

    def drain_halo(which, q):
        for way in range(2):
            @pl.when(narrow != (3 if way == 0 else 0))
            def _():
                halo_copy(which, q, way).wait_send()

    def split_own(field, q):
        def one(i, carry):
            h, l = two_halves(field[q * CHUNK + i])
            at = pl.ds(pl.multiple_of(i * cols, cols), cols)
            e_h[at, LANES:LANES + dofs] = h
            e_l[at, LANES:LANES + dofs] = l
            return carry
        lax.fori_loop(0, CHUNK, one, 0)

    def split_halo(which, q):
        for way in range(2):
            h, l = two_halves(halo[which, way, q])
            at = slice(0, LANES) if way == 0 else slice(LANES + dofs, LANES + dofs + LANES)
            e_h[:, at] = h
            e_l[:, at] = l

    tile = 256

    def apply_own(into_h, into_l):
        def one(j, carry):
            at = pl.ds(pl.multiple_of(j * tile, tile), tile)
            mid = slice(LANES, LANES + dofs)
            p_f[:, at] = dot3(e_h[:, mid], e_l[:, mid], into_h[at, mid], into_l[at, mid])
            return carry
        lax.fori_loop(0, dofs // tile, one, 0)

    def apply_halo(into_h, into_l, done):
        def one(j, carry):
            at = pl.ds(pl.multiple_of(j * tile, tile), tile)
            total = p_f[:, at]
            for side in (slice(0, LANES), slice(LANES + dofs, LANES + dofs + LANES)):
                total = total + dot3(e_h[:, side], e_l[:, side], into_h[at, side], into_l[at, side])
            h, l = two_halves(total)
            done(at, h, l)
            return carry
        lax.fori_loop(0, dofs // tile, one, 0)

    for slot in range(slots):
        arrived(0, slot)
    for q in range(chunks):
        send_halo(vel_in, 0, q)
    for q in range(chunks):
        split_own(vel_in, q)
        apply_own(mass_h, mass_l)
        take_halo(0, q)
        split_halo(0, q)
        at_rows = slice(q * rows, (q + 1) * rows)

        def keep_v(at, h, l):
            v_h[at_rows, at] = h
            v_l[at_rows, at] = l
        apply_halo(mass_h, mass_l, keep_v)

    def core_copy(q):
        return pltpu.make_async_remote_copy(
            src_ref=x_out.at[1 - core, q], dst_ref=x_in.at[q], send_sem=x_send.at[q], recv_sem=x_recv.at[q],
            device_id=core_partner, device_id_type=MESH,
        )

    def y_copy(q):
        return pltpu.make_async_remote_copy(
            src_ref=y_out.at[1 - high_y, q], dst_ref=y_in.at[q], send_sem=y_send.at[q], recv_sem=y_recv.at[q],
            device_id=y_partner, device_id_type=MESH,
        )

    def z_copy(slot):
        return pltpu.make_async_remote_copy(
            src_ref=z_out.at[slot], dst_ref=z_in.at[slot], send_sem=z_send.at[slot], recv_sem=z_recv.at[slot],
            device_id={"wide": back(SHIFTS[slot])}, device_id_type=MESH,
        )

    def products(q):
        for slot in range(q * CHUNK, (q + 1) * CHUNK):
            arrived(1, slot)
        send_halo(pos_in, 1, q)
        split_own(pos_in, q)
        apply_own(stiff_h, stiff_l)
        take_halo(1, q)
        split_halo(1, q)

        def keep_p(at, h, l):
            p_h[:, at] = h
            p_l[:, at] = l
        apply_halo(stiff_h, stiff_l, keep_p)

        def one(j, carry):
            at = pl.ds(pl.multiple_of(j * tile, tile), tile)
            x = dot3(p_h[...], p_l[...], v_h[at, :], v_l[at, :])
            x = x.reshape(CHUNK, 2, 2, 8, tile)
            for c in range(2):
                x_out[c, q, :, :, :, at] = x[:, :, c]
            return carry
        lax.fori_loop(0, v_h.shape[0] // tile, one, 0)
        core_copy(q).start()

    def reduce_core(q):
        core_copy(q).wait_recv()

        def one(i, carry):
            for h in range(2):
                y_out[h, q, i] = x_out[core, q, i, h] + x_in[q, i, h]
            return carry
        lax.fori_loop(0, CHUNK, one, 0)
        y_copy(q).start()

    def reduce_y(q):
        y_copy(q).wait_recv()
        for i in range(CHUNK):
            slot = q * CHUNK + i
            z_out[slot] = y_out[high_y, q, i] + y_in[q, i ^ 1]
            if SHIFTS[slot] != (0, 0, 0):
                z_copy(slot).start()

    for q in range(chunks):
        products(q)
        reduce_core(q)
        reduce_y(q)

    home = SHIFTS.index((0, 0, 0))
    total = z_out[home]
    for slot in range(slots):
        if slot != home:
            z_copy(slot).wait_recv()
            total = total + z_in[slot]
    out_ref[...] = total * scale

    for group in copies:
        for slot in range(slots):
            if slot != home:
                group[slot].wait_send()
    for which in range(2):
        for q in range(chunks):
            drain_halo(which, q)
    for q in range(chunks):
        core_copy(q).wait_send()
        y_copy(q).wait_send()
    for slot in range(slots):
        if slot != home:
            z_copy(slot).wait_send()


def shards(pos_factor, vel_factor, stiff_vals, stiff_pattern, mass_vals, mass_pattern, interface):
    wide, narrow = lax.axis_size("wide"), lax.axis_size("narrow")
    cols = pos_factor.shape[0]
    dofs = pos_factor.shape[1] // wide
    every = cols * wide
    slots = len(SHIFTS)
    chunks = slots // CHUNK
    rows = CHUNK * cols
    extended = dofs + 2 * LANES
    scale = 1.0 / math.sqrt(dofs * wide * narrow)
    f32, b16 = jnp.float32, jnp.bfloat16
    vmem = functools.partial(pl.BlockSpec, memory_space=pltpu.VMEM)
    smem = functools.partial(pl.BlockSpec, memory_space=pltpu.SMEM)
    hbm = functools.partial(pl.BlockSpec, memory_space=pl.ANY)
    dma = pltpu.SemaphoreType.DMA
    return pl.pallas_call(
        functools.partial(kernel, scale),
        out_shape=jax.ShapeDtypeStruct((8, every), f32),
        in_specs=[hbm(), hbm(), vmem(), smem(), vmem(), smem(), smem()],
        out_specs=vmem(),
        scratch_shapes=[
            pltpu.VMEM((slots, cols, dofs), f32),
            pltpu.VMEM((slots, cols, dofs), f32),
            pltpu.VMEM((2, 2, chunks, rows, LANES), f32),
            pltpu.VMEM((2, 2, chunks, rows, LANES), f32),
            pltpu.VMEM((dofs, extended), b16),
            pltpu.VMEM((dofs, extended), b16),
            pltpu.VMEM((dofs, extended), b16),
            pltpu.VMEM((dofs, extended), b16),
            pltpu.VMEM((rows, extended), b16),
            pltpu.VMEM((rows, extended), b16),
            pltpu.VMEM((rows, dofs), f32),
            pltpu.VMEM((rows, dofs), b16),
            pltpu.VMEM((rows, dofs), b16),
            pltpu.VMEM((every, dofs), b16),
            pltpu.VMEM((every, dofs), b16),
            pltpu.VMEM((2, chunks, CHUNK, 2, 8, every), f32),
            pltpu.VMEM((chunks, CHUNK, 2, 8, every), f32),
            pltpu.VMEM((2, chunks, CHUNK, 8, every), f32),
            pltpu.VMEM((chunks, CHUNK, 8, every), f32),
            pltpu.VMEM((slots, 8, every), f32),
            pltpu.VMEM((slots, 8, every), f32),
            dma((2, slots)), dma((2, slots)), dma((2,)),
            dma((2, 2, chunks)), dma((2, 2, chunks)),
            dma((chunks,)), dma((chunks,)),
            dma((chunks,)), dma((chunks,)),
            dma((slots,)), dma((slots,)),
        ],
        compiler_params=pltpu.CompilerParams(
            collective_id=0, has_side_effects=True, vmem_limit_bytes=60 << 20
        ),
    )(pos_factor, vel_factor, stiff_vals, stiff_pattern, mass_vals, mass_pattern, interface)


def solution(mesh):
    return jax.shard_map(
        shards,
        mesh=mesh,
        in_specs=(
            P("wide", "narrow"),
            P("wide", "narrow"),
            P("narrow", "wide", None, None),
            P("narrow", "wide", None),
            P("narrow", "wide", None, None),
            P("narrow", "wide", None),
            P("narrow", "wide", None, None),
        ),
        out_specs=P(("wide", "narrow"), None),
        check_vma=False,
    )
```

```python
import functools
import math

import jax
import jax.numpy as jnp
from jax import lax
from jax.experimental import pallas as pl
from jax.experimental.pallas import tpu as pltpu
from jax.sharding import PartitionSpec as P

MESH = pl.DeviceIdType.MESH
X_SIDE = 4
Z_SIDE = 4
LANES = 128

PAIRS = (
    (1, 1), (3, 3), (2, 0), (0, 2),
    (1, 3), (3, 1), (2, 2), (0, 0),
    (1, 2), (3, 2), (2, 1), (2, 3),
    (3, 0), (1, 0), (0, 3), (0, 1),
)
SHIFTS = tuple((dy, dx, dz) for dx, dz in PAIRS for dy in (0, 1))
CUTS = (0, 8, 16, 24, 32)
WINDOW = 8
LAG = 5
TILE = 256
HOME = SHIFTS.index((0, 0, 0))
NEGATED = tuple(SHIFTS.index((dy, -dx % X_SIDE, -dz % Z_SIDE)) for dy, dx, dz in SHIFTS)


def two_halves(value):
    high = value.astype(jnp.bfloat16)
    low = (value - high.astype(jnp.float32)).astype(jnp.bfloat16)
    return high, low


def dot_t(a, b):
    return lax.dot_general(a, b, (((1,), (1,)), ((), ())), preferred_element_type=jnp.float32)


def dot3(ah, al, bh, bl):
    return dot_t(ah, bh) + (dot_t(ah, bl) + dot_t(al, bh))


def kernel(
    scale, pos_ref, vel_ref, stiff_ref, stiff_pat, mass_ref, mass_pat, picks, out_ref,
    pos_in, vel_in, relay, halo, halo_out, stiff_h, stiff_l, mass_h, mass_l,
    ev_h, ev_l, ep_h, ep_l, v_f, p_f, p_h, p_l, v_h, v_l,
    x_out, x_in, y_out, y_in, z_out, z_in,
    send_sem, recv_sem, own_sem, relay_send, relay_recv, halo_send, halo_recv, x_send, x_recv, y_send, y_recv, z_send, z_recv,
):
    wide = lax.axis_index("wide")
    narrow = lax.axis_index("narrow")
    plane = X_SIDE * Z_SIDE
    me_y, me_x, me_z = wide // plane, (wide // Z_SIDE) % X_SIDE, wide % Z_SIDE
    core, high_y = narrow % 2, narrow // 2
    slots = len(SHIFTS)
    chunks = len(CUTS) - 1
    cols, dofs = pos_in.shape[1], pos_in.shape[2]
    every = slots * cols
    blocks = mass_ref.shape[1]
    size = mass_ref.shape[2]
    tiles = every // TILE

    def at_distance(dy, dx, dz):
        return ((me_y + dy) % 2) * plane + ((me_x + dx + X_SIDE) % X_SIDE) * Z_SIDE + (me_z + dz + Z_SIDE) % Z_SIDE

    sign = 1 - 2 * core

    def target_of(slot):
        dy, dx, dz = SHIFTS[slot]
        return at_distance(dy, sign * dx, sign * dz)

    def source_of(slot):
        dy, dx, dz = SHIFTS[slot]
        return at_distance(dy, -sign * dx, -sign * dz)

    core_partner = {"narrow": narrow + 1 - 2 * core}
    y_partner = {"wide": (wide + plane) % (2 * plane), "narrow": (narrow + 2) % 4}

    barrier = pltpu.get_barrier_semaphore()
    for slot in range(slots):
        if slot != HOME:
            pl.semaphore_signal(barrier, inc=1, device_id={"wide": target_of(slot)}, device_id_type=MESH)
    for step in (1, 2, 3):
        pl.semaphore_signal(barrier, inc=1, device_id={"narrow": (narrow + step) % 4}, device_id_type=MESH)
    pl.semaphore_signal(barrier, inc=1, device_id=y_partner, device_id_type=MESH)
    pl.semaphore_wait(barrier, slots - 1 + 3 + 1)

    pairs = len(PAIRS)
    here = HOME // 2

    def landing(which, slot, owner):
        return vel_in.at[owner] if which == 0 else pos_in.at[slot]

    def block_for(which, target):
        return (vel_ref, pos_ref)[which].at[:, pl.ds(pl.multiple_of(target * dofs, dofs), dofs)]

    across = (wide + plane) % (2 * plane)
    home_copies = [
        pltpu.make_async_copy(block_for(which, wide), landing(which, HOME, wide), own_sem.at[which]) for which in range(2)
    ]

    def along_y(which, k):
        return pltpu.make_async_remote_copy(
            src_ref=block_for(which, target_of(2 * k + 1)),
            dst_ref=landing(which, HOME + 1, wide) if k == here else relay.at[which, k],
            send_sem=relay_send.at[which, k], recv_sem=relay_recv.at[which, k],
            device_id={"wide": across}, device_id_type=MESH,
        )

    def in_plane(which, slot):
        k, far = slot // 2, slot % 2
        target = target_of(2 * k)
        return pltpu.make_async_remote_copy(
            src_ref=relay.at[which, k] if far else block_for(which, target),
            dst_ref=landing(which, slot, across if far else wide),
            send_sem=send_sem.at[which, slot], recv_sem=recv_sem.at[which, slot],
            device_id={"wide": target}, device_id_type=MESH,
        )

    def issue(n):
        if n < 2 * pairs:
            which, k = n // pairs, n % pairs
            along_y(which, k).start()
            if k != here:
                in_plane(which, 2 * k).start()

    def step(n):
        which, k = n // pairs, n % pairs
        along_y(which, k).wait_recv()
        if k != here:
            in_plane(which, 2 * k + 1).start()
        issue(n + WINDOW)

    for which in range(2):
        home_copies[which].start()
    for n in range(WINDOW):
        issue(n)

    def arrived(which, slot):
        if slot == HOME:
            home_copies[which].wait()
        elif slot // 2 != here:
            in_plane(which, slot).wait_recv()

    lane = lax.broadcasted_iota(jnp.int32, (1, LANES), 1)
    left = lane < size
    half = lane // size
    ends = (slice(0, LANES), slice(LANES + dofs, LANES + dofs + LANES))
    middle = slice(LANES, LANES + dofs)

    def build(values, pattern, into_h, into_l):
        def row(b, carry):
            pair_tiles = [values[0, b, :, t * LANES:(t + 1) * LANES] for t in range(2)]
            turned = [pltpu.roll(t, size, 1) for t in pair_tiles]
            twice = []
            for t in range(2):
                twice.append(jnp.where(left, pair_tiles[t], turned[t]))
                twice.append(jnp.where(left, turned[t], pair_tiles[t]))
            at = pl.ds(pl.multiple_of(b * size, size), size)
            for pair in range(into_h.shape[1] // LANES):
                total = jnp.zeros((size, LANES), jnp.float32)
                for k in range(4):
                    total = total + jnp.where(half == pattern[0, k, b] - 2 * pair, twice[k], 0.0)
                h, l = two_halves(total)
                into_h[at, pair * LANES:(pair + 1) * LANES] = h
                into_l[at, pair * LANES:(pair + 1) * LANES] = l
            return carry

        lax.fori_loop(0, blocks, row, 0)

    build(mass_ref, mass_pat, mass_h, mass_l)
    build(stiff_ref, stiff_pat, stiff_h, stiff_l)

    @pl.when(narrow == 0)
    def _():
        halo[:, 0] = jnp.zeros(halo.shape[:1] + halo.shape[2:], jnp.float32)

    @pl.when(narrow == 3)
    def _():
        halo[:, 1] = jnp.zeros(halo.shape[:1] + halo.shape[2:], jnp.float32)

    wanted = [jnp.where(left, picks[0, 0, way, 0], picks[0, 0, way, 1]) for way in range(2)]

    def take_in(which, field, entry, into_h, into_l, at):
        found = [jnp.zeros((cols, LANES), jnp.float32)] * 2
        for t in range(dofs // LANES):
            tile = field[entry, :, t * LANES:(t + 1) * LANES]
            turned = pltpu.roll(tile, size, 1)
            twice = (jnp.where(left, tile, turned), jnp.where(left, turned, tile))
            for way in range(2):
                for h in range(2):
                    found[way] = jnp.where(wanted[way] == 2 * t + h, twice[h], found[way])
            high, low = two_halves(tile)
            into_h[at, LANES + t * LANES:2 * LANES + t * LANES] = high
            into_l[at, LANES + t * LANES:2 * LANES + t * LANES] = low
        for way in range(2):
            halo_out[which, way, entry] = found[way]

    def halo_copy(which, q, way):
        lo, hi = (0, slots) if which == 0 else CUTS[q:q + 2]
        n = 0 if which == 0 else 1 + q
        return pltpu.make_async_remote_copy(
            src_ref=halo_out.at[which, way, lo:hi], dst_ref=halo.at[which, way, lo:hi],
            send_sem=halo_send.at[n, way], recv_sem=halo_recv.at[n, way],
            device_id={"narrow": (narrow + (1 if way == 0 else 3)) % 4}, device_id_type=MESH,
        )

    def send_halo(which, q):
        for way in range(2):
            @pl.when(narrow != (3 if way == 0 else 0))
            def _():
                halo_copy(which, q, way).start()

    def take_halo(which, q):
        for way in range(2):
            @pl.when(narrow != (0 if way == 0 else 3))
            def _():
                halo_copy(which, q, way).wait_recv()

    def drain_halo(which, q):
        for way in range(2):
            @pl.when(narrow != (3 if way == 0 else 0))
            def _():
                halo_copy(which, q, way).wait_send()

    def per_tile(count, body):
        def one(j, carry):
            body(j, pl.ds(pl.multiple_of(j * TILE, TILE), TILE))
            return carry
        lax.fori_loop(0, count, one, 0)

    def split_halo(which, entry, into_h, into_l, at):
        for way in range(2):
            into_h[at, ends[way]], into_l[at, ends[way]] = two_halves(halo[which, way, entry])

    def velocity_first(q):
        rows = slice(q * TILE, (q + 1) * TILE)

        def body(j, at):
            v_f[rows, at] = dot3(ev_h[rows, middle], ev_l[rows, middle], mass_h[at, middle], mass_l[at, middle])
        per_tile(dofs // TILE, body)

    def velocity_second():
        take_halo(0, 0)

        def one(i, carry):
            split_halo(0, i, ev_h, ev_l, pl.ds(pl.multiple_of(i * cols, cols), cols))
            return carry
        lax.fori_loop(0, slots, one, 0)

        def rows_of(q, carry):
            rows = pl.ds(pl.multiple_of(q * TILE, TILE), TILE)

            def body(j, at):
                total = v_f[rows, at]
                for side in ends:
                    total = total + dot3(ev_h[rows, side], ev_l[rows, side], mass_h[at, side], mass_l[at, side])
                v_h[rows, at], v_l[rows, at] = two_halves(total)
            per_tile(dofs // TILE, body)
            return carry
        lax.fori_loop(0, every // TILE, rows_of, 0)

    def core_copy(q, j):
        lo, hi = CUTS[q:q + 2]
        return pltpu.make_async_remote_copy(
            src_ref=x_out.at[1 - core, j, lo:hi], dst_ref=x_in.at[j, lo:hi],
            send_sem=x_send.at[q, j], recv_sem=x_recv.at[q, j], device_id=core_partner, device_id_type=MESH,
        )

    def y_copy(q, j):
        lo, hi = CUTS[q:q + 2]
        return pltpu.make_async_remote_copy(
            src_ref=y_out.at[1 - high_y, j, lo:hi], dst_ref=y_in.at[j, lo:hi],
            send_sem=y_send.at[q, j], recv_sem=y_recv.at[q, j], device_id=y_partner, device_id_type=MESH,
        )

    def z_copy(slot, j):
        at = slice(j * TILE, (j + 1) * TILE)
        return pltpu.make_async_remote_copy(
            src_ref=z_out.at[slot, :, at], dst_ref=z_in.at[slot, :, at],
            send_sem=z_send.at[slot, j], recv_sem=z_recv.at[slot, j],
            device_id={"wide": source_of(slot)}, device_id_type=MESH,
        )

    def rows_at(slot, end):
        return slice(slot * cols, end * cols)

    def position_in(slot):
        arrived(1, slot)
        take_in(1, pos_in, slot, ep_h, ep_l, rows_at(slot, slot + 1))

    def position_halo(q):
        take_halo(1, q)
        for slot in range(*CUTS[q:q + 2]):
            split_halo(1, NEGATED[slot], ep_h, ep_l, rows_at(slot, slot + 1))

    def position_first(q):
        rows = rows_at(*CUTS[q:q + 2])

        def body(j, at):
            p_f[:, at] = dot3(ep_h[rows, middle], ep_l[rows, middle], stiff_h[at, middle], stiff_l[at, middle])
        per_tile(dofs // TILE, body)

    def position_second(q):
        position_halo(q)
        lo, hi = CUTS[q:q + 2]
        rows, into = rows_at(lo, hi), rows_at(0, hi - lo)

        def body(j, at):
            total = p_f[:, at]
            for side in ends:
                total = total + dot3(ep_h[rows, side], ep_l[rows, side], stiff_h[at, side], stiff_l[at, side])
            p_h[into, at], p_l[into, at] = two_halves(total)
        per_tile(dofs // TILE, body)

    def product_tile(q, j, at):
        lo, hi = CUTS[q:q + 2]
        rows = rows_at(0, hi - lo)
        x = dot3(p_h[rows, :], p_l[rows, :], v_h[at, :], v_l[at, :])
        x = x.reshape(hi - lo, 2, 2, 8, TILE)
        for c in range(2):
            x_out[c, j, lo:hi] = x[:, :, c]
        core_copy(q, j).start()

    def core_tile(q, j):
        core_copy(q, j).wait_recv()
        for slot in range(*CUTS[q:q + 2]):
            for h in range(2):
                y_out[h, j, slot] = x_out[core, j, slot, h] + x_in[j, NEGATED[slot], h]
        y_copy(q, j).start()

    def products(q):
        per_tile(tiles, functools.partial(product_tile, q))

    def reduce_core(q):
        def one(j, carry):
            core_tile(q, j)
            return carry
        lax.fori_loop(0, tiles, one, 0)

    def products_and_reduce(q):
        def one(j, carry):
            product_tile(q, j, pl.ds(pl.multiple_of(j * TILE, TILE), TILE))

            @pl.when(j > 0)
            def _():
                core_tile(q, j - 1)
            return carry
        lax.fori_loop(0, tiles, one, 0)
        core_tile(q, tiles - 1)

    def reduce_y(q):
        for j in range(tiles):
            y_copy(q, j).wait_recv()
            for slot in range(*CUTS[q:q + 2]):
                z_out[slot, :, j * TILE:(j + 1) * TILE] = y_out[high_y, j, slot] + y_in[j, slot ^ 1]
                if slot != HOME:
                    z_copy(slot, j).start()

    def velocity_in(k):
        for slot in (2 * k, 2 * k + 1):
            arrived(0, slot)
            source = source_of(slot)
            take_in(0, vel_in, source, ev_h, ev_l, pl.ds(pl.multiple_of(source * cols, cols), cols))

    pending = list(range(2 * pairs))

    def steps(count):
        for _ in range(count):
            if pending:
                step(pending.pop(0))

    def chunk_in(q):
        for slot in range(*CUTS[q:q + 2]):
            position_in(slot)
        send_halo(1, q)

    steps(LAG)
    for k in range(pairs):
        steps(1)
        velocity_in(k)
    send_halo(0, 0)
    for q in range(every // TILE):
        velocity_first(q)
        steps(1)
    chunk_in(0)
    steps(2)
    velocity_second()
    steps(2)
    position_first(0)
    chunk_in(1)
    for q in range(2, chunks):
        steps(2)
        position_second(q - 2)
        products(q - 2)
        if q > 2:
            reduce_core(q - 3)
        steps(2)
        position_first(q - 1)
        chunk_in(q)
    steps(2 * pairs)
    last = chunks - 1
    position_second(last - 1)
    products(last - 1)
    reduce_core(last - 2)
    reduce_y(last - 3)
    position_first(last)
    reduce_core(last - 1)
    reduce_y(last - 2)
    position_second(last)
    products_and_reduce(last)
    reduce_y(last - 1)
    reduce_y(last)

    for j in range(tiles):
        at = slice(j * TILE, (j + 1) * TILE)
        total = z_out[HOME, :, at]
        for slot in range(slots):
            if slot != HOME:
                z_copy(slot, j).wait_recv()
                total = total + z_in[slot, :, at]
        out_ref[:, at] = total * scale

    for which in range(2):
        for k in range(pairs):
            along_y(which, k).wait_send()
            if k != here:
                in_plane(which, 2 * k).wait_send()
                in_plane(which, 2 * k + 1).wait_send()
    drain_halo(0, 0)
    for q in range(chunks):
        drain_halo(1, q)
        for j in range(tiles):
            core_copy(q, j).wait_send()
            y_copy(q, j).wait_send()
    for slot in range(slots):
        if slot != HOME:
            for j in range(tiles):
                z_copy(slot, j).wait_send()


def shards(pos_factor, vel_factor, stiff_vals, stiff_pattern, mass_vals, mass_pattern, interface):
    wide, narrow = lax.axis_size("wide"), lax.axis_size("narrow")
    cols = pos_factor.shape[0]
    dofs = pos_factor.shape[1] // wide
    every = cols * wide
    slots = len(SHIFTS)
    chunks = len(CUTS) - 1
    rows = max(hi - lo for lo, hi in zip(CUTS, CUTS[1:])) * cols
    tiles = every // TILE
    extended = dofs + 2 * LANES
    scale = 1.0 / math.sqrt(dofs * wide * narrow)
    f32, b16 = jnp.float32, jnp.bfloat16
    vmem = functools.partial(pl.BlockSpec, memory_space=pltpu.VMEM)
    smem = functools.partial(pl.BlockSpec, memory_space=pltpu.SMEM)
    hbm = functools.partial(pl.BlockSpec, memory_space=pl.ANY)
    dma = pltpu.SemaphoreType.DMA
    return pl.pallas_call(
        functools.partial(kernel, scale),
        out_shape=jax.ShapeDtypeStruct((8, every), f32),
        in_specs=[hbm(), hbm(), vmem(), smem(), vmem(), smem(), smem()],
        out_specs=vmem(),
        scratch_shapes=[
            pltpu.VMEM((slots, cols, dofs), f32),
            pltpu.VMEM((slots, cols, dofs), f32),
            pltpu.VMEM((2, len(PAIRS), cols, dofs), f32),
            pltpu.VMEM((2, 2, slots, cols, LANES), f32),
            pltpu.VMEM((2, 2, slots, cols, LANES), f32),
            pltpu.VMEM((dofs, extended), b16),
            pltpu.VMEM((dofs, extended), b16),
            pltpu.VMEM((dofs, extended), b16),
            pltpu.VMEM((dofs, extended), b16),
            pltpu.VMEM((every, extended), b16),
            pltpu.VMEM((every, extended), b16),
            pltpu.VMEM((every, extended), b16),
            pltpu.VMEM((every, extended), b16),
            pltpu.VMEM((every, dofs), f32),
            pltpu.VMEM((rows, dofs), f32),
            pltpu.VMEM((rows, dofs), b16),
            pltpu.VMEM((rows, dofs), b16),
            pltpu.VMEM((every, dofs), b16),
            pltpu.VMEM((every, dofs), b16),
            pltpu.VMEM((2, tiles, slots, 2, 8, TILE), f32),
            pltpu.VMEM((tiles, slots, 2, 8, TILE), f32),
            pltpu.VMEM((2, tiles, slots, 8, TILE), f32),
            pltpu.VMEM((tiles, slots, 8, TILE), f32),
            pltpu.VMEM((slots, 8, every), f32),
            pltpu.VMEM((slots, 8, every), f32),
            dma((2, slots)), dma((2, slots)), dma((2,)),
            dma((2, len(PAIRS))), dma((2, len(PAIRS))),
            dma((1 + chunks, 2)), dma((1 + chunks, 2)),
            dma((chunks, tiles)), dma((chunks, tiles)),
            dma((chunks, tiles)), dma((chunks, tiles)),
            dma((slots, tiles)), dma((slots, tiles)),
        ],
        compiler_params=pltpu.CompilerParams(
            collective_id=0, has_side_effects=True, vmem_limit_bytes=63 << 20
        ),
    )(
        pos_factor, vel_factor, stiff_vals, jnp.swapaxes(stiff_pattern, 1, 2),
        mass_vals, jnp.swapaxes(mass_pattern, 1, 2), interface,
    )


def solution(mesh):
    return jax.shard_map(
        shards,
        mesh=mesh,
        in_specs=(
            P("wide", "narrow"),
            P("wide", "narrow"),
            P("narrow", "wide", None, None),
            P("narrow", "wide", None),
            P("narrow", "wide", None, None),
            P("narrow", "wide", None),
            P("narrow", "wide", None, None),
        ),
        out_specs=P(("wide", "narrow"), None),
        check_vma=False,
    )
```

```python
import functools
import math

import jax
import jax.numpy as jnp
from jax import lax
from jax.experimental import pallas as pl
from jax.experimental.pallas import tpu as pltpu
from jax.sharding import PartitionSpec as P

MESH = pl.DeviceIdType.MESH
X_SIDE = 4
Z_SIDE = 4
LANES = 128

PAIRS = (
    (1, 1), (3, 3), (2, 0), (0, 2),
    (1, 3), (3, 1), (2, 2), (0, 0),
    (1, 2), (3, 2), (2, 1), (2, 3),
    (3, 0), (1, 0), (0, 3), (0, 1),
)
SHIFTS = tuple((dy, dx, dz) for dx, dz in PAIRS for dy in (0, 1))
CUTS = (0, 8, 16, 24, 32)
WINDOW = 6
LAG = 5
TILE = 256
HOME = SHIFTS.index((0, 0, 0))
NEGATED = tuple(SHIFTS.index((dy, -dx % X_SIDE, -dz % Z_SIDE)) for dy, dx, dz in SHIFTS)


def two_halves(value):
    high = value.astype(jnp.bfloat16)
    low = (value - high.astype(jnp.float32)).astype(jnp.bfloat16)
    return high, low


def dot_t(a, b):
    return lax.dot_general(a, b, (((1,), (1,)), ((), ())), preferred_element_type=jnp.float32)


def dot3(ah, al, bh, bl):
    return dot_t(ah, bh) + (dot_t(ah, bl) + dot_t(al, bh))


def kernel(
    scale, pos_ref, vel_ref, stiff_ref, stiff_pat, mass_ref, mass_pat, picks, out_ref,
    pos_in, vel_in, relay, halo, halo_out, stiff_h, stiff_l, mass_h, mass_l,
    ev_h, ev_l, ep_h, ep_l, v_f, p_f, p_h, p_l, v_h, v_l,
    x_out, x_in, y_out, y_in, z_out, z_in,
    send_sem, recv_sem, own_sem, relay_send, relay_recv, halo_send, halo_recv, x_send, x_recv, y_send, y_recv, z_send, z_recv,
):
    wide = lax.axis_index("wide")
    narrow = lax.axis_index("narrow")
    plane = X_SIDE * Z_SIDE
    me_y, me_x, me_z = wide // plane, (wide // Z_SIDE) % X_SIDE, wide % Z_SIDE
    core, high_y = narrow % 2, narrow // 2
    slots = len(SHIFTS)
    chunks = len(CUTS) - 1
    cols, dofs = pos_in.shape[1], pos_in.shape[2]
    every = slots * cols
    blocks = mass_ref.shape[1]
    size = mass_ref.shape[2]
    tiles = every // TILE

    def at_distance(dy, dx, dz):
        return ((me_y + dy) % 2) * plane + ((me_x + dx + X_SIDE) % X_SIDE) * Z_SIDE + (me_z + dz + Z_SIDE) % Z_SIDE

    sign = 1 - 2 * core

    def target_of(slot):
        dy, dx, dz = SHIFTS[slot]
        return at_distance(dy, sign * dx, sign * dz)

    def source_of(slot):
        dy, dx, dz = SHIFTS[slot]
        return at_distance(dy, -sign * dx, -sign * dz)

    core_partner = {"narrow": narrow + 1 - 2 * core}
    y_partner = {"wide": (wide + plane) % (2 * plane), "narrow": (narrow + 2) % 4}

    barrier = pltpu.get_barrier_semaphore()
    for slot in range(slots):
        if slot != HOME:
            pl.semaphore_signal(barrier, inc=1, device_id={"wide": target_of(slot)}, device_id_type=MESH)
    for step in (1, 2, 3):
        pl.semaphore_signal(barrier, inc=1, device_id={"narrow": (narrow + step) % 4}, device_id_type=MESH)
    pl.semaphore_signal(barrier, inc=1, device_id=y_partner, device_id_type=MESH)
    pl.semaphore_wait(barrier, slots - 1 + 3 + 1)

    pairs = len(PAIRS)
    here = HOME // 2

    def landing(which, slot, owner):
        return vel_in.at[owner] if which == 0 else pos_in.at[slot]

    def block_for(which, target):
        return (vel_ref, pos_ref)[which].at[:, pl.ds(pl.multiple_of(target * dofs, dofs), dofs)]

    across = (wide + plane) % (2 * plane)
    home_copies = [
        pltpu.make_async_copy(block_for(which, wide), landing(which, HOME, wide), own_sem.at[which]) for which in range(2)
    ]

    def along_y(which, k):
        return pltpu.make_async_remote_copy(
            src_ref=block_for(which, target_of(2 * k + 1)),
            dst_ref=landing(which, HOME + 1, wide) if k == here else relay.at[which, k],
            send_sem=relay_send.at[which, k], recv_sem=relay_recv.at[which, k],
            device_id={"wide": across}, device_id_type=MESH,
        )

    def in_plane(which, slot):
        k, far = slot // 2, slot % 2
        target = target_of(2 * k)
        return pltpu.make_async_remote_copy(
            src_ref=relay.at[which, k] if far else block_for(which, target),
            dst_ref=landing(which, slot, across if far else wide),
            send_sem=send_sem.at[which, slot], recv_sem=recv_sem.at[which, slot],
            device_id={"wide": target}, device_id_type=MESH,
        )

    def issue(n):
        if n < 2 * pairs:
            which, k = n // pairs, n % pairs
            along_y(which, k).start()
            if k != here:
                in_plane(which, 2 * k).start()

    def step(n):
        which, k = n // pairs, n % pairs
        along_y(which, k).wait_recv()
        if k != here:
            in_plane(which, 2 * k + 1).start()
        issue(n + WINDOW)

    for which in range(2):
        home_copies[which].start()
    for n in range(WINDOW):
        issue(n)

    def arrived(which, slot):
        if slot == HOME:
            home_copies[which].wait()
        elif slot // 2 != here:
            in_plane(which, slot).wait_recv()

    lane = lax.broadcasted_iota(jnp.int32, (1, LANES), 1)
    left = lane < size
    half = lane // size
    ends = (slice(0, LANES), slice(LANES + dofs, LANES + dofs + LANES))
    middle = slice(LANES, LANES + dofs)

    def build(values, pattern, into_h, into_l):
        def row(b, carry):
            pair_tiles = [values[0, b, :, t * LANES:(t + 1) * LANES] for t in range(2)]
            turned = [pltpu.roll(t, size, 1) for t in pair_tiles]
            twice = []
            for t in range(2):
                twice.append(jnp.where(left, pair_tiles[t], turned[t]))
                twice.append(jnp.where(left, turned[t], pair_tiles[t]))
            at = pl.ds(pl.multiple_of(b * size, size), size)
            for pair in range(into_h.shape[1] // LANES):
                total = jnp.zeros((size, LANES), jnp.float32)
                for k in range(4):
                    total = total + jnp.where(half == pattern[0, k, b] - 2 * pair, twice[k], 0.0)
                h, l = two_halves(total)
                into_h[at, pair * LANES:(pair + 1) * LANES] = h
                into_l[at, pair * LANES:(pair + 1) * LANES] = l
            return carry

        lax.fori_loop(0, blocks, row, 0)

    build(mass_ref, mass_pat, mass_h, mass_l)
    build(stiff_ref, stiff_pat, stiff_h, stiff_l)

    @pl.when(narrow == 0)
    def _():
        halo[:, 0] = jnp.zeros(halo.shape[:1] + halo.shape[2:], jnp.float32)

    @pl.when(narrow == 3)
    def _():
        halo[:, 1] = jnp.zeros(halo.shape[:1] + halo.shape[2:], jnp.float32)

    wanted = [jnp.where(left, picks[0, 0, way, 0], picks[0, 0, way, 1]) for way in range(2)]

    def take_in(which, field, entry, into_h, into_l, at):
        found = [jnp.zeros((cols, LANES), jnp.float32)] * 2
        for t in range(dofs // LANES):
            tile = field[entry, :, t * LANES:(t + 1) * LANES]
            turned = pltpu.roll(tile, size, 1)
            twice = (jnp.where(left, tile, turned), jnp.where(left, turned, tile))
            for way in range(2):
                for h in range(2):
                    found[way] = jnp.where(wanted[way] == 2 * t + h, twice[h], found[way])
            high, low = two_halves(tile)
            into_h[at, LANES + t * LANES:2 * LANES + t * LANES] = high
            into_l[at, LANES + t * LANES:2 * LANES + t * LANES] = low
        for way in range(2):
            halo_out[which, way, entry] = found[way]

    def halo_copy(which, n, way, view):
        return pltpu.make_async_remote_copy(
            src_ref=halo_out.at[which, way, view], dst_ref=halo.at[which, way, view],
            send_sem=halo_send.at[n, way], recv_sem=halo_recv.at[n, way],
            device_id={"narrow": (narrow + (1 if way == 0 else 3)) % 4}, device_id_type=MESH,
        )

    def halo_copies(which, q, way):
        if which == 0:
            return [halo_copy(0, slot, way, slice(slot, slot + 1)) for slot in range(slots)]
        return [halo_copy(1, slots + q, way, slice(*CUTS[q:q + 2]))]

    def send_block_halo(slot, entry):
        for way in range(2):
            @pl.when(narrow != (3 if way == 0 else 0))
            def _():
                halo_copy(0, slot, way, pl.ds(entry, 1)).start()

    def send_halo(which, q):
        for way in range(2):
            @pl.when(narrow != (3 if way == 0 else 0))
            def _():
                for copy in halo_copies(which, q, way):
                    copy.start()

    def take_halo(which, q):
        for way in range(2):
            @pl.when(narrow != (0 if way == 0 else 3))
            def _():
                for copy in halo_copies(which, q, way):
                    copy.wait_recv()

    def drain_halo(which, q):
        for way in range(2):
            @pl.when(narrow != (3 if way == 0 else 0))
            def _():
                for copy in halo_copies(which, q, way):
                    copy.wait_send()

    def per_tile(count, body):
        def one(j, carry):
            body(j, pl.ds(pl.multiple_of(j * TILE, TILE), TILE))
            return carry
        lax.fori_loop(0, count, one, 0)

    def split_halo(which, entry, into_h, into_l, at):
        for way in range(2):
            into_h[at, ends[way]], into_l[at, ends[way]] = two_halves(halo[which, way, entry])

    def velocity_first(q):
        rows = slice(q * TILE, (q + 1) * TILE)

        def body(j, at):
            v_f[rows, at] = dot3(ev_h[rows, middle], ev_l[rows, middle], mass_h[at, middle], mass_l[at, middle])
        per_tile(dofs // TILE, body)

    def velocity_second():
        take_halo(0, 0)

        def one(i, carry):
            split_halo(0, i, ev_h, ev_l, pl.ds(pl.multiple_of(i * cols, cols), cols))
            return carry
        lax.fori_loop(0, slots, one, 0)

        def rows_of(q, carry):
            rows = pl.ds(pl.multiple_of(q * TILE, TILE), TILE)

            def body(j, at):
                total = v_f[rows, at]
                for side in ends:
                    total = total + dot3(ev_h[rows, side], ev_l[rows, side], mass_h[at, side], mass_l[at, side])
                v_h[rows, at], v_l[rows, at] = two_halves(total)
            per_tile(dofs // TILE, body)
            return carry
        lax.fori_loop(0, every // TILE, rows_of, 0)

    def core_copy(q, j):
        lo, hi = CUTS[q:q + 2]
        return pltpu.make_async_remote_copy(
            src_ref=x_out.at[1 - core, j, lo:hi], dst_ref=x_in.at[j, lo:hi],
            send_sem=x_send.at[q, j], recv_sem=x_recv.at[q, j], device_id=core_partner, device_id_type=MESH,
        )

    def y_copy(q, j):
        lo, hi = CUTS[q:q + 2]
        return pltpu.make_async_remote_copy(
            src_ref=y_out.at[1 - high_y, j, lo:hi], dst_ref=y_in.at[j, lo:hi],
            send_sem=y_send.at[q, j], recv_sem=y_recv.at[q, j], device_id=y_partner, device_id_type=MESH,
        )

    def z_copy(slot, j):
        at = slice(j * TILE, (j + 1) * TILE)
        return pltpu.make_async_remote_copy(
            src_ref=z_out.at[slot, :, at], dst_ref=z_in.at[slot, :, at],
            send_sem=z_send.at[slot, j], recv_sem=z_recv.at[slot, j],
            device_id={"wide": source_of(slot)}, device_id_type=MESH,
        )

    def rows_at(slot, end):
        return slice(slot * cols, end * cols)

    def position_in(slot):
        arrived(1, slot)
        take_in(1, pos_in, slot, ep_h, ep_l, rows_at(slot, slot + 1))

    def position_halo(q):
        take_halo(1, q)
        for slot in range(*CUTS[q:q + 2]):
            split_halo(1, NEGATED[slot], ep_h, ep_l, rows_at(slot, slot + 1))

    def position_first(q):
        rows = rows_at(*CUTS[q:q + 2])

        def body(j, at):
            p_f[:, at] = dot3(ep_h[rows, middle], ep_l[rows, middle], stiff_h[at, middle], stiff_l[at, middle])
        per_tile(dofs // TILE, body)

    def position_second(q):
        position_halo(q)
        lo, hi = CUTS[q:q + 2]
        rows, into = rows_at(lo, hi), rows_at(0, hi - lo)

        def body(j, at):
            total = p_f[:, at]
            for side in ends:
                total = total + dot3(ep_h[rows, side], ep_l[rows, side], stiff_h[at, side], stiff_l[at, side])
            p_h[into, at], p_l[into, at] = two_halves(total)
        per_tile(dofs // TILE, body)

    def product_tile(q, j, at):
        lo, hi = CUTS[q:q + 2]
        rows = rows_at(0, hi - lo)
        x = dot3(p_h[rows, :], p_l[rows, :], v_h[at, :], v_l[at, :])
        x = x.reshape(hi - lo, 2, 2, 8, TILE)
        for c in range(2):
            x_out[c, j, lo:hi] = x[:, :, c]
        core_copy(q, j).start()

    def core_tile(q, j):
        core_copy(q, j).wait_recv()
        for slot in range(*CUTS[q:q + 2]):
            for h in range(2):
                y_out[h, j, slot] = x_out[core, j, slot, h] + x_in[j, NEGATED[slot], h]
        y_copy(q, j).start()

    def products(q):
        per_tile(tiles, functools.partial(product_tile, q))

    def reduce_core(q):
        def one(j, carry):
            core_tile(q, j)
            return carry
        lax.fori_loop(0, tiles, one, 0)

    def products_and_reduce(q):
        def one(j, carry):
            product_tile(q, j, pl.ds(pl.multiple_of(j * TILE, TILE), TILE))

            @pl.when(j > 0)
            def _():
                core_tile(q, j - 1)
            return carry
        lax.fori_loop(0, tiles, one, 0)
        core_tile(q, tiles - 1)

    def reduce_y(q):
        for j in range(tiles):
            y_copy(q, j).wait_recv()
            for slot in range(*CUTS[q:q + 2]):
                z_out[slot, :, j * TILE:(j + 1) * TILE] = y_out[high_y, j, slot] + y_in[j, slot ^ 1]
                if slot != HOME:
                    z_copy(slot, j).start()

    def velocity_in(k):
        for slot in (2 * k, 2 * k + 1):
            arrived(0, slot)
            source = source_of(slot)
            take_in(0, vel_in, source, ev_h, ev_l, pl.ds(pl.multiple_of(source * cols, cols), cols))
            send_block_halo(slot, source)

    pending = list(range(2 * pairs))

    def steps(count):
        for _ in range(count):
            if pending:
                step(pending.pop(0))

    def chunk_in(q):
        for slot in range(*CUTS[q:q + 2]):
            position_in(slot)
        send_halo(1, q)

    steps(LAG)
    for k in range(pairs):
        steps(1)
        velocity_in(k)
    for q in range(every // TILE):
        velocity_first(q)
        steps(1)
    chunk_in(0)
    steps(2)
    velocity_second()
    steps(2)
    position_first(0)
    chunk_in(1)
    for q in range(2, chunks):
        steps(2)
        position_second(q - 2)
        products(q - 2)
        if q > 2:
            reduce_core(q - 3)
        steps(2)
        position_first(q - 1)
        chunk_in(q)
    steps(2 * pairs)
    last = chunks - 1
    position_second(last - 1)
    products(last - 1)
    reduce_core(last - 2)
    reduce_y(last - 3)
    position_first(last)
    reduce_core(last - 1)
    reduce_y(last - 2)
    position_second(last)
    products_and_reduce(last)
    reduce_y(last - 1)
    reduce_y(last)

    for j in range(tiles):
        at = slice(j * TILE, (j + 1) * TILE)
        total = z_out[HOME, :, at]
        for slot in range(slots):
            if slot != HOME:
                z_copy(slot, j).wait_recv()
                total = total + z_in[slot, :, at]
        out_ref[:, at] = total * scale

    for which in range(2):
        for k in range(pairs):
            along_y(which, k).wait_send()
            if k != here:
                in_plane(which, 2 * k).wait_send()
                in_plane(which, 2 * k + 1).wait_send()
    drain_halo(0, 0)
    for q in range(chunks):
        drain_halo(1, q)
        for j in range(tiles):
            core_copy(q, j).wait_send()
            y_copy(q, j).wait_send()
    for slot in range(slots):
        if slot != HOME:
            for j in range(tiles):
                z_copy(slot, j).wait_send()


def shards(pos_factor, vel_factor, stiff_vals, stiff_pattern, mass_vals, mass_pattern, interface):
    wide, narrow = lax.axis_size("wide"), lax.axis_size("narrow")
    cols = pos_factor.shape[0]
    dofs = pos_factor.shape[1] // wide
    every = cols * wide
    slots = len(SHIFTS)
    chunks = len(CUTS) - 1
    rows = max(hi - lo for lo, hi in zip(CUTS, CUTS[1:])) * cols
    tiles = every // TILE
    extended = dofs + 2 * LANES
    scale = 1.0 / math.sqrt(dofs * wide * narrow)
    f32, b16 = jnp.float32, jnp.bfloat16
    vmem = functools.partial(pl.BlockSpec, memory_space=pltpu.VMEM)
    smem = functools.partial(pl.BlockSpec, memory_space=pltpu.SMEM)
    hbm = functools.partial(pl.BlockSpec, memory_space=pl.ANY)
    dma = pltpu.SemaphoreType.DMA
    return pl.pallas_call(
        functools.partial(kernel, scale),
        out_shape=jax.ShapeDtypeStruct((8, every), f32),
        in_specs=[hbm(), hbm(), vmem(), smem(), vmem(), smem(), smem()],
        out_specs=vmem(),
        scratch_shapes=[
            pltpu.VMEM((slots, cols, dofs), f32),
            pltpu.VMEM((slots, cols, dofs), f32),
            pltpu.VMEM((2, len(PAIRS), cols, dofs), f32),
            pltpu.VMEM((2, 2, slots, cols, LANES), f32),
            pltpu.VMEM((2, 2, slots, cols, LANES), f32),
            pltpu.VMEM((dofs, extended), b16),
            pltpu.VMEM((dofs, extended), b16),
            pltpu.VMEM((dofs, extended), b16),
            pltpu.VMEM((dofs, extended), b16),
            pltpu.VMEM((every, extended), b16),
            pltpu.VMEM((every, extended), b16),
            pltpu.VMEM((every, extended), b16),
            pltpu.VMEM((every, extended), b16),
            pltpu.VMEM((every, dofs), f32),
            pltpu.VMEM((rows, dofs), f32),
            pltpu.VMEM((rows, dofs), b16),
            pltpu.VMEM((rows, dofs), b16),
            pltpu.VMEM((every, dofs), b16),
            pltpu.VMEM((every, dofs), b16),
            pltpu.VMEM((2, tiles, slots, 2, 8, TILE), f32),
            pltpu.VMEM((tiles, slots, 2, 8, TILE), f32),
            pltpu.VMEM((2, tiles, slots, 8, TILE), f32),
            pltpu.VMEM((tiles, slots, 8, TILE), f32),
            pltpu.VMEM((slots, 8, every), f32),
            pltpu.VMEM((slots, 8, every), f32),
            dma((2, slots)), dma((2, slots)), dma((2,)),
            dma((2, len(PAIRS))), dma((2, len(PAIRS))),
            dma((slots + chunks, 2)), dma((slots + chunks, 2)),
            dma((chunks, tiles)), dma((chunks, tiles)),
            dma((chunks, tiles)), dma((chunks, tiles)),
            dma((slots, tiles)), dma((slots, tiles)),
        ],
        compiler_params=pltpu.CompilerParams(
            collective_id=0, has_side_effects=True, vmem_limit_bytes=63 << 20
        ),
    )(
        pos_factor, vel_factor, stiff_vals, jnp.swapaxes(stiff_pattern, 1, 2),
        mass_vals, jnp.swapaxes(mass_pattern, 1, 2), interface,
    )


def solution(mesh):
    return jax.shard_map(
        shards,
        mesh=mesh,
        in_specs=(
            P("wide", "narrow"),
            P("wide", "narrow"),
            P("narrow", "wide", None, None),
            P("narrow", "wide", None),
            P("narrow", "wide", None, None),
            P("narrow", "wide", None),
            P("narrow", "wide", None, None),
        ),
        out_specs=P(("wide", "narrow"), None),
        check_vma=False,
    )
```
